32 devices in a mesh: sub: 4 (over y, x), row: 8 (over z, core).
Axes of the slice: x: 2, y: 2, z: 4, core: 2. Of those that a mesh axis runs over, the one named last changes fastest.
Arguments:
- inverse: float32 [4, 1024, 12288], P('sub', 'row')
- sources: float32 [4, 16, 12288], P('sub', None, 'row'), may hold values from -6 to 6
- line_history: float32 [4, 32, 1024], P('sub', None, 'row'), may hold values from -6 to 6
- line_dest: int32 [4, 1024], P('sub', 'row'), may hold values from 0 to 3, as said below
- line_port: int32 [4, 1024], P('sub', 'row'), may hold values from 0 to 1023
- line_delay: int32 [4, 1024], P('sub', 'row'), may hold values from 16 to 32
- prev_voltage: float32 [4, 1024], P('sub', 'row'), may hold values from -6 to 6
- flux_start: float32 [4, 1024], P('sub', 'row'), may hold values from -3 to 3
- arrester_gain: float32 [4, 1024], P('sub', 'row'), may hold values from 0.5 to 4
- core_gain: float32 [4, 1024], P('sub', 'row'), may hold values from 0.25 to 2
- arrester_slots: int32 [4, 128], P('sub', 'row'), may hold values from 0 to 127, as said below
- core_slots: int32 [4, 128], P('sub', 'row'), may hold values from 0 to 127, as said below
Outputs:
- voltages: float32 [4, 16, 1024], P('sub', None, 'row')
- final_flux: float32 [4, 1024], P('sub', 'row')
The draws below stay inside these ranges and needn't reach their ends.
Inputs may be any that keep to these rules, and one draw needn't show every extreme that they name: `line_dest`: a record never names its own subnetwork; among the 128 records of one device no subnetwork is named more than 86 times, and in every such block some subnetwork is named exactly 86 times. `arrester_slots`: the 16 entries of one device are distinct slots of that device's 128 ports and share no slot with that device's core entries. `core_slots`: the 16 entries of one device are distinct slots of that device's 128 ports.
All inputs are finite; a program needn't handle non-finite values.
Results may differ from the reference program's by a relative error of at most 0.0003.
Values sent between devices are 32-bit elements; how exact they have to be, the bound alone decides.
A program may use at most 64 MiB of HBM per device.

```python
import math
import jax
import jax.numpy as jnp
from jax import lax

ORDER = 12288
PORT_DEV = 128
LINE_DEV = 128
STEPS = 16
HISTORY = 32
NEWTON = 2
ARREST_DEV = 16
CORE_DEV = 16
SUBNETWORK_COUNT = 4
PORTS = 1024
SLICE = 1536
LINES = 1024
CAPACITY = 86
ARRESTERS = 128
CORES = 128


def line_tables(key):
    base_key = jax.random.fold_in(key, 11)
    row_count = LINES // LINE_DEV
    blocks = SUBNETWORK_COUNT * row_count
    total_options = (SUBNETWORK_COUNT - 1) * CAPACITY

    def one_block(index):
        block_random_key = jax.random.fold_in(base_key, index)
        extra_score_key, forced_pick_key, jitter_key, port_random_key, delay_random_key = jax.random.split(block_random_key, 5)
        owner = index // row_count
        remaining_items = jnp.arange(total_options, dtype=jnp.int32) // CAPACITY
        extra_score = jax.random.randint(extra_score_key, (SUBNETWORK_COUNT - 1,), 0, 3)
        forced_pick = jax.random.randint(forced_pick_key, (), 0, SUBNETWORK_COUNT - 1)
        extra_score = jnp.where(jnp.arange(SUBNETWORK_COUNT - 1, dtype=jnp.int32) == forced_pick, 8, extra_score)
        random_jitter = jax.random.randint(jitter_key, (total_options,), 0, 1024)
        ranking_scores = (extra_score[remaining_items] * 1024 + random_jitter) * 1024 + jnp.arange(total_options, dtype=jnp.int32)
        ignored, chosen = lax.top_k(ranking_scores, LINE_DEV)
        picked = remaining_items[chosen]
        target = picked + (picked >= owner).astype(jnp.int32)
        target_port = jax.random.randint(port_random_key, (LINE_DEV,), 0, PORTS)
        travel = jax.random.randint(delay_random_key, (LINE_DEV,), STEPS, HISTORY + 1)
        return (target.astype(jnp.int32), target_port.astype(jnp.int32), travel.astype(jnp.int32))
    target, target_port, travel = jax.vmap(one_block)(jnp.arange(blocks, dtype=jnp.int32))
    return (target.reshape(SUBNETWORK_COUNT, LINES), target_port.reshape(SUBNETWORK_COUNT, LINES), travel.reshape(SUBNETWORK_COUNT, LINES))


def draw_line_dest(key, part):
    return line_tables(key)[0]


def draw_line_port(key, part):
    return line_tables(key)[1]


def draw_line_delay(key, part):
    return line_tables(key)[2]


def slot_tables(key):
    base_key = jax.random.fold_in(key, 23)
    blocks = SUBNETWORK_COUNT * (PORTS // PORT_DEV)

    def one_block(index):
        ordering = jax.random.permutation(jax.random.fold_in(base_key, index), PORT_DEV).astype(jnp.int32)
        return (ordering[:ARREST_DEV], ordering[ARREST_DEV:ARREST_DEV + CORE_DEV])
    arrest_part, core_part = jax.vmap(one_block)(jnp.arange(blocks, dtype=jnp.int32))
    return (arrest_part.reshape(SUBNETWORK_COUNT, ARRESTERS), core_part.reshape(SUBNETWORK_COUNT, CORES))


def draw_arrester_slots(key, part):
    return slot_tables(key)[0]


def draw_core_slots(key, part):
    return slot_tables(key)[1]


def draw_inverse(key, part):
    base_key = jax.random.fold_in(key, 31)
    key_body, key_diag = jax.random.split(base_key)
    spread = jax.random.normal(key_body, (SUBNETWORK_COUNT, PORTS, ORDER), jnp.float32) * (0.7 / math.sqrt(ORDER))
    diagonal = jnp.exp(jax.random.uniform(key_diag, (SUBNETWORK_COUNT, PORTS), jnp.float32, math.log(0.3), 0.0))
    port_iota = jnp.arange(PORTS, dtype=jnp.int32)
    node_of = port_iota // PORT_DEV * SLICE + port_iota % PORT_DEV
    on_diagonal = node_of[:, None] == jnp.arange(ORDER, dtype=jnp.int32)[None, :]
    return jnp.where(on_diagonal[None, :, :], diagonal[:, :, None], spread)


def level_of(key, dims, cuts, smallest, high):
    factor_of, own = 1.0, jax.random.fold_in(key, 6)
    for axis_at, shards_of in cuts:
        draws = jnp.exp(jax.random.uniform(jax.random.fold_in(own, axis_at), (shards_of,), jnp.float32, smallest / len(cuts), high / len(cuts)))
        factor_of = factor_of * jnp.repeat(draws, dims[axis_at] // shards_of).reshape([-1 if axis == axis_at else 1 for axis in range(len(dims))])
    return factor_of


def gaussian(rng, dims, scale, bound, cuts=(), kind=jnp.bfloat16):
    loudness = level_of(rng, dims, cuts, -0.22, 0.18) if cuts else 1.0
    drawn = jax.random.normal(rng, dims, jnp.float32) * scale * loudness
    return jnp.minimum(jnp.maximum(drawn, -bound), bound).astype(kind)


def setup_inputs(seed: int = 0) -> dict:
    arg_keys = jax.random.split(jax.random.key(seed), 13)
    return {
        "inverse": draw_inverse(jax.random.fold_in(arg_keys[12], 71), 0),
        "sources": gaussian(arg_keys[1], (SUBNETWORK_COUNT, STEPS, ORDER), 1.0, 6.0, ((0, 4), (2, 8)), jnp.float32),
        "line_history": gaussian(arg_keys[2], (SUBNETWORK_COUNT, HISTORY, LINES), 1.0, 6.0, ((0, 4), (2, 8)), jnp.float32),
        "line_dest": draw_line_dest(jax.random.fold_in(arg_keys[12], 71), 0),
        "line_port": draw_line_port(jax.random.fold_in(arg_keys[12], 71), 0),
        "line_delay": draw_line_delay(jax.random.fold_in(arg_keys[12], 71), 0),
        "prev_voltage": gaussian(arg_keys[6], (SUBNETWORK_COUNT, PORTS), 1.0, 6.0, ((0, 4), (1, 8)), jnp.float32),
        "flux_start": gaussian(arg_keys[7], (SUBNETWORK_COUNT, PORTS), 0.5, 3.0, ((0, 4), (1, 8)), jnp.float32),
        "arrester_gain": jnp.clip(jnp.exp(math.log(4.0) - 2.0794415 * jax.random.uniform(arg_keys[8], (SUBNETWORK_COUNT, PORTS), jnp.float32) ** level_of(arg_keys[8], (SUBNETWORK_COUNT, PORTS), ((0, 4), (1, 8)), -0.2, 0.2)), 0.5, 4.0),
        "core_gain": jnp.clip(jnp.exp(math.log(2.0) - 2.0794415 * jax.random.uniform(arg_keys[9], (SUBNETWORK_COUNT, PORTS), jnp.float32) ** level_of(arg_keys[9], (SUBNETWORK_COUNT, PORTS), ((0, 4), (1, 8)), -0.2, 0.2)), 0.25, 2.0),
        "arrester_slots": draw_arrester_slots(jax.random.fold_in(arg_keys[12], 71), 0),
        "core_slots": draw_core_slots(jax.random.fold_in(arg_keys[12], 71), 0),
    }


half_step = 0.25
knee_volts = 1.5
cubic_term = 0.25


def slot_mask(slots, per_block):
    entries = slots.shape[1]
    port_of = (jnp.arange(entries, dtype=jnp.int32) // per_block) * PORT_DEV + slots
    hits = port_of[:, :, None] == jnp.arange(PORTS, dtype=jnp.int32)[None, None, :]
    return jnp.any(hits, axis=1).astype(jnp.float32)


def element_terms(iterate, voltage, flux_now, arrester_mask, arrester_gain, core_mask, core_gain):
    linked = flux_now + half_step * (iterate + voltage)
    ratio = iterate / knee_volts
    current = arrester_mask * arrester_gain * iterate * (1.0 + ratio * ratio) + core_mask * core_gain * (linked + cubic_term * linked * linked * linked)
    slope_now = arrester_mask * arrester_gain * (1.0 + 3.0 * ratio * ratio) + core_mask * core_gain * half_step * (1.0 + 3.0 * cubic_term * linked * linked)
    return current, slope_now


def reference(inverse, sources, line_history, line_dest, line_port, line_delay, prev_voltage, flux_start, arrester_gain, core_gain, arrester_slots, core_slots):
    row_count = PORTS // PORT_DEV
    records = SUBNETWORK_COUNT * LINES
    flat_hist = jnp.transpose(line_history, (1, 0, 2)).reshape(HISTORY, records)
    delays = line_delay.reshape(records)
    lag_index = HISTORY + jnp.arange(STEPS, dtype=jnp.int32)[:, None] - delays[None, :]
    picked = jnp.take_along_axis(flat_hist, lag_index, axis=0)
    segment = (line_dest * PORTS + line_port).reshape(records)
    summed = jax.ops.segment_sum(picked.T, segment, num_segments=SUBNETWORK_COUNT * PORTS)
    history = -jnp.transpose(summed.reshape(SUBNETWORK_COUNT, PORTS, STEPS), (0, 2, 1))
    padded = jnp.pad(history.reshape(SUBNETWORK_COUNT, STEPS, row_count, PORT_DEV), ((0, 0), (0, 0), (0, 0), (0, SLICE - PORT_DEV)))
    injection = sources + padded.reshape(SUBNETWORK_COUNT, STEPS, ORDER)
    linear = jnp.einsum("spn,stn->stp", inverse, injection, precision=lax.Precision.HIGHEST)
    coupling = inverse.reshape(SUBNETWORK_COUNT, PORTS, row_count, SLICE)[:, :, :, :PORT_DEV].reshape(SUBNETWORK_COUNT, PORTS, PORTS)
    self_imp = jnp.diagonal(coupling, axis1=1, axis2=2)
    arrester_mask = slot_mask(arrester_slots, ARREST_DEV)
    core_mask = slot_mask(core_slots, CORE_DEV)

    def advance(carried, linear_now):
        voltage, flux_now = carried
        iterate = voltage
        for newton_pass in range(NEWTON):
            current, slope_now = element_terms(iterate, voltage, flux_now, arrester_mask, arrester_gain, core_mask, core_gain)
            network = linear_now - jnp.einsum("spq,sq->sp", coupling, current, precision=lax.Precision.HIGHEST)
            iterate = iterate - (iterate - network) / (1.0 + self_imp * slope_now)
        return (iterate, flux_now + half_step * (iterate + voltage)), iterate

    (last_voltage, final_flux), stacked = lax.scan(advance, (prev_voltage, flux_start), jnp.transpose(linear, (1, 0, 2)))
    return jnp.transpose(stacked, (1, 0, 2)), final_flux
```

```python
import functools

import jax
import jax.numpy as jnp
from jax import lax
from jax.experimental import pallas as pl
from jax.experimental.pallas import tpu as pltpu
from jax.sharding import PartitionSpec as P

STEPS = 16
HISTORY = 32
NEWTON = 2
CHUNKS = 2
LANES = 128

half_step = 0.25
knee_volts = 1.5
cubic_term = 0.25

F32 = jnp.float32
BF16 = jnp.bfloat16
MESH = pl.DeviceIdType.MESH
NN = (((1,), (0,)), ((), ()))
NT = (((1,), (1,)), ((), ()))
HIGHEST = lax.Precision.HIGHEST


def iota(shape, axis):
    return lax.broadcasted_iota(jnp.int32, shape, axis)


def hi_lo(x):
    high = x.astype(BF16)
    return high, (x - high.astype(F32)).astype(BF16)


def stack_hi_lo(x):
    return jnp.concatenate(hi_lo(x), axis=0)


def dot(a, b, dims=NN):
    return lax.dot_general(a, b, dims, preferred_element_type=F32)


def four_terms(r):
    n, m = r.shape[0] // 2, r.shape[1] // 2
    return (r[:n, :m] + r[n:, :m]) + (r[:n, m:] + r[n:, m:])


def kernel(
    subs, rows, ports, slice_len, arrests, cores,
    inv, src, hist, dest, port, delay, prev, flux, again, cgain, aslots, cslots,
    out, fout,
    m32, m2, gath, rec, elem, par, fst, recout, x2, wc, fall, vo, cu, acc, hacc,
    inv_sem, src_sem, line_send, line_recv, rec_send, rec_recv, par_send, par_recv,
    elem_send, elem_recv, fst_send, fst_recv,
):
    s = lax.axis_index("sub")
    me = lax.axis_index("row")
    z, c = me // 2, me % 2
    zn = rows // 2
    partner = z * 2 + (1 - c)
    elems = arrests + cores
    group = LANES // elems
    total = rows * elems
    halves = total // LANES
    width = slice_len // CHUNKS

    barrier = pltpu.get_barrier_semaphore()
    for j in range(1, rows):
        pl.semaphore_signal(barrier, inc=1, device_id=(s, lax.rem(me + j, rows)), device_id_type=MESH)
    for j in range(1, subs):
        pl.semaphore_signal(barrier, inc=1, device_id=(lax.rem(s + j, subs), me), device_id_type=MESH)

    for k in range(CHUNKS):
        pltpu.make_async_copy(
            src.at[0, :, pl.ds(k * width, width)], gath.at[k, me], src_sem.at[k]
        ).start()

    def inv_copy(r):
        cols = pl.ds(pl.multiple_of(r * slice_len, LANES), slice_len)
        return pltpu.make_async_copy(inv.at[0, :, cols], m32.at[:, cols], inv_sem.at[r])

    for r in range(rows):
        inv_copy(r).start()

    shifted = hist[0]
    shift = HISTORY - delay[...]
    bit = 1
    while bit <= HISTORY - STEPS:
        moved = pltpu.roll(shifted, HISTORY - bit, 0)
        shifted = jnp.where((shift // bit) % 2 == 1, moved, shifted)
        bit *= 2
    recout[:STEPS, :] = shifted[:STEPS, :]
    recout[STEPS:, :] = jnp.broadcast_to((dest[...] * (rows * ports) + port[...]).astype(F32), (8, LANES))

    lane16a, row16a = iota((arrests, LANES), 1), iota((arrests, LANES), 0)
    lane16c, row16c = iota((cores, LANES), 1), iota((cores, LANES), 0)
    put_a = jnp.where(lane16a % elems == row16a, 1.0, 0.0).astype(BF16)
    put_c = jnp.where(lane16c % elems == row16c + arrests, 1.0, 0.0).astype(BF16)
    slot_a = jnp.broadcast_to(aslots[...].astype(F32), (8, arrests)).astype(BF16)
    slot_c = jnp.broadcast_to(cslots[...].astype(F32), (8, cores)).astype(BF16)
    slot_row = (dot(slot_a, put_a) + dot(slot_c, put_c))[0:1, :]
    hit = iota((ports, LANES), 0).astype(F32) == slot_row
    slot_tiled = jnp.where(hit, 1.0, 0.0)
    slot_own = jnp.where(iota((ports, LANES), 1) // elems == me % group, slot_tiled, 0.0)
    r8 = iota((8, ports), 0)
    params = jnp.where(
        r8 == 0,
        iota((8, ports), 1).astype(F32),
        jnp.where(
            r8 == 1,
            again[...],
            jnp.where(r8 == 2, cgain[...], jnp.where(r8 == 3, prev[...], flux[...])),
        ),
    )
    par[me] = lax.dot_general(params, slot_own, NN, precision=HIGHEST, preferred_element_type=F32)

    pl.semaphore_wait(barrier, rows + subs - 2)

    def line_copy(kind, b, way, target):
        ref = rec.at[b] if kind == CHUNKS else gath.at[kind, b]
        return pltpu.make_async_remote_copy(
            src_ref=ref, dst_ref=ref, send_sem=line_send.at[kind, b, way],
            recv_sem=line_recv.at[kind, b], device_id=(s, target), device_id_type=MESH,
        )

    def own_sends(kind):
        @pl.when(z + 1 < zn)
        def _():
            line_copy(kind, me, 0, me + 2).start()

        @pl.when(z > 0)
        def _():
            line_copy(kind, me, 1, me - 2).start()

        line_copy(kind, me, 2, partner).start()

    for j in range(1, subs):
        to = lax.rem(s + j, subs)
        pltpu.make_async_remote_copy(
            src_ref=recout, dst_ref=rec.at[me, subs - 1 - j], send_sem=rec_send.at[j - 1],
            recv_sem=rec_recv.at[subs - 1 - j], device_id=(to, me), device_id_type=MESH,
        ).start()
    for j in range(1, rows):
        pltpu.make_async_remote_copy(
            src_ref=par.at[me], dst_ref=par.at[me], send_sem=par_send.at[j - 1],
            recv_sem=par_recv.at[me], device_id=(s, lax.rem(me + j, rows)), device_id_type=MESH,
        ).start()
    for k in range(CHUNKS):
        pltpu.make_async_copy(
            src.at[0, :, pl.ds(k * width, width)], gath.at[k, me], src_sem.at[k]
        ).wait()
        own_sends(k)

    def split_matrix(r, carry):
        inv_copy(r).wait()
        cols = pl.ds(pl.multiple_of(r * slice_len, LANES), slice_len)
        high, low = hi_lo(m32[:, cols])
        m2[:ports, cols] = high
        m2[ports:, cols] = low
        return carry

    early = min(2, rows)
    lax.fori_loop(0, early, split_matrix, 0)

    for j in range(subs - 1):
        pltpu.make_async_remote_copy(
            src_ref=recout, dst_ref=rec.at[me, j], send_sem=rec_send.at[j],
            recv_sem=rec_recv.at[j], device_id=(s, me), device_id_type=MESH,
        ).wait_recv()
    own_sends(CHUNKS)
    lax.fori_loop(early, rows, split_matrix, 0)

    for j in range(1, rows):
        b = lax.rem(me + j, rows)
        pltpu.make_async_remote_copy(
            src_ref=par.at[b], dst_ref=par.at[b], send_sem=par_send.at[j - 1],
            recv_sem=par_recv.at[b], device_id=(s, b), device_id_type=MESH,
        ).wait_recv()
    all_par = jnp.concatenate(
        [sum(par[h * group + i] for i in range(group)) for h in range(halves)], axis=1
    )
    slots_all = all_par[0:1, :]
    at_slot = iota((ports, total), 0).astype(F32) == slots_all
    owner_of = iota((ports, total), 1) // elems
    pick = None
    for r in range(rows):
        choose = jnp.where(jnp.logical_and(at_slot, owner_of == r), 1.0, 0.0).astype(BF16)
        term = dot(m2[:, r * slice_len : r * slice_len + ports], choose)
        pick = term if pick is None else pick + term
    x2[...] = pick.astype(BF16)
    slot_cols = jnp.transpose(slot_tiled)[:elems].astype(BF16)
    elem[me] = dot(slot_cols, x2[:ports, :]) + dot(slot_cols, x2[ports:, :])

    def elem_copy(b, sem_at, target):
        return pltpu.make_async_remote_copy(
            src_ref=elem.at[b], dst_ref=elem.at[b], send_sem=elem_send.at[sem_at],
            recv_sem=elem_recv.at[b], device_id=(s, target), device_id_type=MESH,
        )

    for j in range(1, zn):
        elem_copy(me, zn + j - 1, lax.rem(z + j, zn) * 2 + c).start()
    elem_copy(me, z, partner).start()

    acc[...] = jnp.zeros_like(acc)
    hacc[...] = jnp.zeros_like(hacc)
    base = s * (rows * ports)

    def use_sources(b, kind):
        cols = pl.ds(pl.multiple_of(b * slice_len + kind * width, LANES), width)
        acc[...] += dot(stack_hi_lo(gath[kind, b]), m2[:, cols], NT)

    def use_records(b):
        values = jnp.concatenate([rec[b, j, :STEPS, :] for j in range(subs - 1)], axis=1)
        keys = jnp.concatenate([rec[b, j, STEPS : STEPS + 1, :] for j in range(subs - 1)], axis=1)
        packed = stack_hi_lo(values)

        def one(r, carry):
            ids = (iota((ports, (subs - 1) * LANES), 0) + (base + r * ports)).astype(F32)
            land = jnp.where(ids == keys, 1.0, 0.0).astype(BF16)
            hacc[r] += dot(packed, land, NT)
            return carry

        lax.fori_loop(0, rows, one, 0)

    def use(b):
        for k in range(CHUNKS):
            use_sources(b, k)
        use_records(b)

    use(me)
    for k in range(CHUNKS + 1):
        line_copy(k, partner, 2, partner).wait_recv()
    use(partner)

    def ring(i, carry):
        below = i % 2 == 0
        k = i // 2 + 1
        zb = jnp.where(below, z - k, z + k)
        zt = jnp.where(below, z + 1, z - 1)
        b = zb * 2 + c

        @pl.when(jnp.logical_and(zb >= 0, zb < zn))
        def _():
            for kind in range(CHUNKS + 1):
                line_copy(kind, b, 0, partner).wait_recv()

                @pl.when(jnp.logical_and(zt >= 0, zt < zn))
                def _():
                    line_copy(kind, b, 0, zt * 2 + c).start()

                line_copy(kind, b, 2, partner).start()
            use(b)
            other = zb * 2 + (1 - c)
            for kind in range(CHUNKS + 1):
                line_copy(kind, other, 2, partner).wait_recv()
            use(other)

        return carry

    lax.fori_loop(0, 2 * (zn - 1), ring, 0)

    tot = acc[...]
    for r in range(rows):
        landed = hacc[r]
        landed = landed[:STEPS] + landed[STEPS:]
        tot = tot - dot(stack_hi_lo(landed), m2[:, r * slice_len : r * slice_len + ports], NT)
    first = four_terms(tot)
    fst[me] = lax.dot_general(first, slot_own, NN, precision=HIGHEST, preferred_element_type=F32)

    def fst_copy(b, at, target):
        return pltpu.make_async_remote_copy(
            src_ref=fst.at[b], dst_ref=fst.at[b], send_sem=fst_send.at[at],
            recv_sem=fst_recv.at[b], device_id=(s, target), device_id_type=MESH,
        )

    for j in range(1, rows):
        fst_copy(me, j - 1, lax.rem(me + j, rows)).start()

    for j in range(1, zn):
        zb = lax.rem(z + j, zn)
        elem_copy(zb * 2 + c, 0, partner).wait_recv()
        elem_copy(zb * 2 + c, zb, partner).start()
    for j in range(zn):
        elem_copy(lax.rem(z + j, zn) * 2 + (1 - c), 0, partner).wait_recv()

    w = elem[...].reshape(total, total)
    self_row = jnp.sum(jnp.where(iota((total, total), 0) == iota((total, total), 1), w, 0.0), axis=0, keepdims=True)
    w_hi, w_lo = hi_lo(jnp.transpose(w))
    wc[:, :total] = w_hi
    wc[:, total:] = w_lo

    full = (8, total)
    is_arrest = iota(full, 1) % elems < arrests
    arrest_gain = jnp.where(is_arrest, jnp.broadcast_to(all_par[1:2, :], full), 0.0)
    core_gain = jnp.where(is_arrest, 0.0, jnp.broadcast_to(all_par[2:3, :], full))
    elem_self = jnp.broadcast_to(self_row, full)
    volts0 = jnp.broadcast_to(all_par[3:4, :], full)
    flux0 = jnp.broadcast_to(all_par[4:5, :], full)

    for j in range(1, rows):
        fst_copy(lax.rem(me + j, rows), j - 1, partner).wait_recv()
    fall[...] = jnp.concatenate(
        [sum(fst[h * group + i] for i in range(group)) for h in range(halves)], axis=1
    )

    def advance(t, carry):
        voltage, flux_now = carry
        first_now = jnp.broadcast_to(fall[pl.ds(t, 1), :], full)
        iterate = voltage
        for newton_pass in range(NEWTON):
            linked = flux_now + half_step * (iterate + voltage)
            ratio = iterate * (1.0 / knee_volts)
            rr = ratio * ratio
            ll = linked * linked
            current = arrest_gain * (iterate * (1.0 + rr)) + core_gain * (linked * (1.0 + cubic_term * ll))
            slope = arrest_gain * (1.0 + 3.0 * rr) + core_gain * (half_step + (half_step * 3.0 * cubic_term) * ll)
            recip = 1.0 / (1.0 + elem_self * slope)
            got = dot(stack_hi_lo(current), wc[...])
            coupled = got[:8, :total] + got[8:, :total] + got[:8, total:]
            iterate = iterate - (iterate - first_now + coupled) * recip
        vo[pl.ds(t, 1), :] = iterate[0:1]
        cu[pl.ds(t, 1), :] = current[0:1]
        return iterate, flux_now + half_step * (iterate + voltage)

    lax.fori_loop(0, STEPS, advance, (volts0, flux0))

    reach = four_terms(dot(stack_hi_lo(cu[...]), x2[...], NT))
    put = jnp.where(jnp.logical_and(at_slot, owner_of == me), 1.0, 0.0)
    placed = lax.dot_general(vo[...], put, NT, precision=HIGHEST, preferred_element_type=F32)
    here = lax.dot_general(jnp.ones((8, total), BF16), put.astype(BF16), NT, preferred_element_type=F32)[0:1]
    stacked = jnp.where(here > 0.5, placed, first - reach)
    out[0] = stacked
    summed = jnp.sum(stacked, axis=0, keepdims=True)
    fout[...] = flux[...] + half_step * (prev[...] + 2.0 * summed - stacked[STEPS - 1 : STEPS])

    for k in range(CHUNKS + 1):
        @pl.when(z + 1 < zn)
        def _():
            line_copy(k, me, 0, partner).wait_send()

        @pl.when(z > 0)
        def _():
            line_copy(k, me, 1, partner).wait_send()

        line_copy(k, me, 2, partner).wait_send()

    def drain(i, carry):
        below = i % 2 == 0
        k = i // 2 + 1
        zb = jnp.where(below, z - k, z + k)
        zt = jnp.where(below, z + 1, z - 1)
        b = zb * 2 + c

        @pl.when(jnp.logical_and(zb >= 0, zb < zn))
        def _():
            for kind in range(CHUNKS + 1):
                @pl.when(jnp.logical_and(zt >= 0, zt < zn))
                def _():
                    line_copy(kind, b, 0, partner).wait_send()

                line_copy(kind, b, 2, partner).wait_send()

        return carry

    lax.fori_loop(0, 2 * (zn - 1), drain, 0)
    for j in range(1, subs):
        pltpu.make_async_remote_copy(
            src_ref=recout, dst_ref=rec.at[me, subs - 1 - j], send_sem=rec_send.at[j - 1],
            recv_sem=rec_recv.at[subs - 1 - j], device_id=(lax.rem(s + j, subs), me), device_id_type=MESH,
        ).wait_send()
    for j in range(1, rows):
        pltpu.make_async_remote_copy(
            src_ref=par.at[me], dst_ref=par.at[me], send_sem=par_send.at[j - 1],
            recv_sem=par_recv.at[me], device_id=(s, partner), device_id_type=MESH,
        ).wait_send()
        fst_copy(me, j - 1, partner).wait_send()
    for j in range(1, zn):
        elem_copy(me, zn + j - 1, partner).wait_send()
    for j in range(zn):
        elem_copy(lax.rem(z + j, zn) * 2 + c, lax.rem(z + j, zn), partner).wait_send()


def on_device(subs, rows, *args):
    inverse, sources = args[0], args[1]
    ports = inverse.shape[1]
    order = inverse.shape[2]
    slice_len = sources.shape[2]
    arrests, cores = args[10].shape[1], args[11].shape[1]
    elems = arrests + cores
    total = rows * elems
    zn = rows // 2
    vmem = pl.BlockSpec(memory_space=pltpu.VMEM)
    hbm = pl.BlockSpec(memory_space=pl.ANY)
    dma = pltpu.SemaphoreType.DMA
    return pl.pallas_call(
        functools.partial(kernel, subs, rows, ports, slice_len, arrests, cores),
        out_shape=(
            jax.ShapeDtypeStruct((1, STEPS, ports), F32),
            jax.ShapeDtypeStruct((1, ports), F32),
        ),
        in_specs=[hbm, hbm] + [vmem] * 10,
        out_specs=(vmem, vmem),
        scratch_shapes=[
            pltpu.VMEM((ports, order), F32),
            pltpu.VMEM((2 * ports, order), BF16),
            pltpu.VMEM((CHUNKS, rows, STEPS, slice_len // CHUNKS), F32),
            pltpu.VMEM((rows, subs - 1, STEPS + 8, LANES), F32),
            pltpu.VMEM((rows, elems, total), F32),
            pltpu.VMEM((rows, 8, LANES), F32),
            pltpu.VMEM((rows, STEPS, LANES), F32),
            pltpu.VMEM((STEPS + 8, LANES), F32),
            pltpu.VMEM((2 * ports, total), BF16),
            pltpu.VMEM((total, 2 * total), BF16),
            pltpu.VMEM((STEPS, total), F32),
            pltpu.VMEM((STEPS, total), F32),
            pltpu.VMEM((STEPS, total), F32),
            pltpu.VMEM((2 * STEPS, 2 * ports), F32),
            pltpu.VMEM((rows, 2 * STEPS, ports), F32),
            dma((rows,)),
            dma((CHUNKS,)),
            dma((CHUNKS + 1, rows, 3)),
            dma((CHUNKS + 1, rows)),
            dma((subs - 1,)),
            dma((subs - 1,)),
            dma((rows - 1,)),
            dma((rows,)),
            dma((2 * zn - 1,)),
            dma((rows,)),
            dma((rows - 1,)),
            dma((rows,)),
        ],
        compiler_params=pltpu.CompilerParams(collective_id=0, has_side_effects=True),
        name="window",
    )(*args)


def solution(mesh):
    subs, rows = mesh.shape["sub"], mesh.shape["row"]
    in_specs = (
        P("sub", "row", None),
        P("sub", None, "row"),
        P("sub", None, "row"),
    ) + (P("sub", "row"),) * 9
    out_specs = (P("sub", None, "row"), P("sub", "row"))
    return jax.shard_map(
        functools.partial(on_device, subs, rows),
        mesh=mesh, in_specs=in_specs, out_specs=out_specs, check_vma=False,
    )
```

```python
import functools

import jax
import jax.numpy as jnp
from jax import lax
from jax.experimental import pallas as pl
from jax.experimental.pallas import tpu as pltpu
from jax.sharding import PartitionSpec as P

STEPS = 16
HISTORY = 32
NEWTON = 2
CHUNKS = 2
LANES = 128

half_step = 0.25
knee_volts = 1.5
cubic_term = 0.25

F32 = jnp.float32
BF16 = jnp.bfloat16
MESH = pl.DeviceIdType.MESH
NN = (((1,), (0,)), ((), ()))
NT = (((1,), (1,)), ((), ()))
HIGHEST = lax.Precision.HIGHEST


def iota(shape, axis):
    return lax.broadcasted_iota(jnp.int32, shape, axis)


def hi_lo(x):
    high = x.astype(BF16)
    return high, (x - high.astype(F32)).astype(BF16)


def stack_hi_lo(x):
    return jnp.concatenate(hi_lo(x), axis=0)


def dot(a, b, dims=NN):
    return lax.dot_general(a, b, dims, preferred_element_type=F32)


def four_terms(r):
    n, m = r.shape[0] // 2, r.shape[1] // 2
    return (r[:n, :m] + r[n:, :m]) + (r[:n, m:] + r[n:, m:])


def kernel(
    subs, rows, ports, slice_len, arrests, cores, n_small,
    inv, src, *refs,
):
    small_hbm, refs = refs[:n_small], refs[n_small:]
    out, refs = refs[0], refs[1:]
    small, refs = refs[:n_small], refs[n_small:]
    (
        m32, mp32, mp2, gath, recin, rec, elem, par, fst, recout, x2, wc, fall, vo, cu, acc, hacc,
        small_sem, inv_sem, mp_sem, src_sem, line_send, line_recv, sub_send, sub_recv,
        rec_send, rec_recv, par_send, par_recv, elem_send, elem_recv, fst_send, fst_recv,
    ) = refs
    hist, dest, port, delay, prev, flux, again, cgain, aslots, cslots = small
    s = lax.axis_index("sub")
    me = lax.axis_index("row")
    z, c = me // 2, me % 2
    zn = rows // 2
    partner = z * 2 + (1 - c)
    elems = arrests + cores
    group = LANES // elems
    total = rows * elems
    halves = total // LANES
    width = slice_len // CHUNKS
    peers = subs - 1
    turns = 2 * (zn - 1)

    barrier = pltpu.get_barrier_semaphore()
    for j in range(1, rows):
        pl.semaphore_signal(barrier, inc=1, device_id=(s, lax.rem(me + j, rows)), device_id_type=MESH)
    for j in range(1, subs):
        pl.semaphore_signal(barrier, inc=1, device_id=(lax.rem(s + j, subs), me), device_id_type=MESH)

    small_copies = [
        pltpu.make_async_copy(small_hbm[i], small[i], small_sem.at[i]) for i in range(n_small)
    ]
    for copy in small_copies:
        copy.start()

    def src_copy(k):
        return pltpu.make_async_copy(
            src.at[0, :, pl.ds(k * width, width)], gath.at[k, me], src_sem.at[k]
        )

    for k in range(CHUNKS):
        src_copy(k).start()

    def mp_copy(r):
        return pltpu.make_async_copy(
            inv.at[0, :, pl.ds(r * slice_len, ports)], mp32.at[:, pl.ds(r * ports, ports)], mp_sem.at[r]
        )

    for r in range(rows):
        mp_copy(r).start()

    def inv_copy(b):
        cols = pl.ds(pl.multiple_of(b * slice_len, LANES), slice_len)
        return pltpu.make_async_copy(inv.at[0, :, cols], m32.at[:, cols], inv_sem.at[b])

    steps_z = [0]
    for j in range(1, zn):
        hop = (j + 1) // 2
        steps_z.append(hop if j % 2 == 1 else zn - hop)
    for hop in steps_z:
        zb = lax.rem(z + hop, zn)
        inv_copy(zb * 2 + c).start()
        inv_copy(zb * 2 + (1 - c)).start()

    for copy in small_copies:
        copy.wait()

    shifted = hist[0]
    shift = HISTORY - delay[...]
    bit = 1
    while bit <= HISTORY - STEPS:
        moved = pltpu.roll(shifted, HISTORY - bit, 0)
        shifted = jnp.where((shift // bit) % 2 == 1, moved, shifted)
        bit *= 2
    recout[:STEPS, :] = shifted[:STEPS, :]
    k8 = iota((8, LANES), 0)
    tags = jnp.where(k8 == 0, dest[...], jnp.where(k8 == 1, port[...] // ports, port[...] % ports))
    recout[STEPS:, :] = tags.astype(F32)

    lane16a, row16a = iota((arrests, LANES), 1), iota((arrests, LANES), 0)
    lane16c, row16c = iota((cores, LANES), 1), iota((cores, LANES), 0)
    put_a = jnp.where(lane16a % elems == row16a, 1.0, 0.0).astype(BF16)
    put_c = jnp.where(lane16c % elems == row16c + arrests, 1.0, 0.0).astype(BF16)
    slot_a = jnp.broadcast_to(aslots[...].astype(F32), (8, arrests)).astype(BF16)
    slot_c = jnp.broadcast_to(cslots[...].astype(F32), (8, cores)).astype(BF16)
    slot_row = (dot(slot_a, put_a) + dot(slot_c, put_c))[0:1, :]
    hit = iota((ports, LANES), 0).astype(F32) == slot_row
    slot_tiled = jnp.where(hit, 1.0, 0.0)
    slot_own = jnp.where(iota((ports, LANES), 1) // elems == me % group, slot_tiled, 0.0)
    r8 = iota((8, ports), 0)
    params = jnp.where(
        r8 == 0,
        iota((8, ports), 1).astype(F32),
        jnp.where(
            r8 == 1,
            again[...],
            jnp.where(r8 == 2, cgain[...], jnp.where(r8 == 3, prev[...], flux[...])),
        ),
    )
    par[me] = lax.dot_general(params, slot_own, NN, precision=HIGHEST, preferred_element_type=F32)

    for k in range(CHUNKS):
        src_copy(k).wait()
    pl.semaphore_wait(barrier, rows + subs - 2)

    def remote(ref_from, ref_to, send, recv, to_sub, to_row):
        return pltpu.make_async_remote_copy(
            src_ref=ref_from, dst_ref=ref_to, send_sem=send, recv_sem=recv,
            device_id=(to_sub, to_row), device_id_type=MESH,
        )

    def sub_copy(j):
        return remote(
            recout, recin.at[peers - j], sub_send.at[j - 1], sub_recv.at[peers - j],
            lax.rem(s + j, subs), me,
        )

    def par_copy(b, at, target):
        return remote(par.at[b], par.at[b], par_send.at[at], par_recv.at[b], s, target)

    def line_copy(kind, b, way, target):
        ref = gath.at[kind, b]
        return remote(ref, ref, line_send.at[kind, b, way], line_recv.at[kind, b], s, target)

    def rec_copy(b, at, target):
        return remote(rec.at[b], rec.at[b], rec_send.at[at], rec_recv.at[b], s, target)

    def elem_copy(b, at, target):
        return remote(elem.at[b], elem.at[b], elem_send.at[at], elem_recv.at[b], s, target)

    def fst_copy(b, at, target):
        return remote(fst.at[b], fst.at[b], fst_send.at[at], fst_recv.at[b], s, target)

    for j in range(1, subs):
        sub_copy(j).start()
    for j in range(1, rows):
        par_copy(me, j - 1, lax.rem(me + j, rows)).start()
    for k in range(CHUNKS):
        @pl.when(z + 1 < zn)
        def _():
            line_copy(k, me, 0, me + 2).start()

        @pl.when(z > 0)
        def _():
            line_copy(k, me, 1, me - 2).start()

        line_copy(k, me, 2, partner).start()

    for r in range(rows):
        mp_copy(r).wait()
    mp_hi, mp_lo = hi_lo(mp32[...])
    mp2[:ports, :] = mp_hi
    mp2[ports:, :] = mp_lo
    acc[...] = jnp.zeros_like(acc)
    hacc[...] = jnp.zeros_like(hacc)

    for j in range(1, subs):
        sub_copy(j).wait_recv()
    for j in range(peers):
        rec[me, j * STEPS : (j + 1) * STEPS, :] = recin[j, :STEPS, :]
    named = [
        jnp.where(
            recin[j, STEPS : STEPS + 1, :] == s.astype(F32), recin[j, STEPS + 1 : STEPS + 2, :], -1.0
        )
        for j in range(peers)
    ]
    spots = [recin[j, STEPS + 2 : STEPS + 3, :] for j in range(peers)]
    for j, row in enumerate(named + spots):
        rec[me, peers * STEPS + j : peers * STEPS + j + 1, :] = row
    for j in range(1, zn):
        rec_copy(me, zn + j - 1, lax.rem(z + j, zn) * 2 + c).start()
    rec_copy(me, z, partner).start()

    def turn(i):
        below = i % 2 == 0
        k = i // 2 + 1
        zb = jnp.where(below, z - k, z + k)
        zt = jnp.where(below, z + 1, z - 1)
        return zb, zt, jnp.logical_and(zb >= 0, zb < zn), jnp.logical_and(zt >= 0, zt < zn)

    def forward(i, carry):
        zb, zt, valid, onward = turn(i)
        b = zb * 2 + c

        @pl.when(valid)
        def _():
            for kind in range(CHUNKS):
                line_copy(kind, b, 0, partner).wait_recv()

                @pl.when(onward)
                def _():
                    line_copy(kind, b, 0, zt * 2 + c).start()

                line_copy(kind, b, 2, partner).start()

        return carry

    lax.fori_loop(0, 2, forward, 0)

    for j in range(1, rows):
        par_copy(lax.rem(me + j, rows), j - 1, partner).wait_recv()
    all_par = jnp.concatenate(
        [sum(par[h * group + i] for i in range(group)) for h in range(halves)], axis=1
    )
    slots_all = all_par[0:1, :]
    at_slot = iota((ports, total), 0).astype(F32) == slots_all
    owner_of = iota((ports, total), 1) // elems
    pick = None
    for r in range(rows):
        choose = jnp.where(jnp.logical_and(at_slot, owner_of == r), 1.0, 0.0).astype(BF16)
        term = dot(mp2[:, r * ports : (r + 1) * ports], choose)
        pick = term if pick is None else pick + term
    x2[...] = pick.astype(BF16)
    slot_cols = jnp.transpose(slot_tiled)[:elems].astype(BF16)
    elem[me] = dot(slot_cols, x2[:ports, :]) + dot(slot_cols, x2[ports:, :])
    for j in range(1, zn):
        elem_copy(me, zn + j - 1, lax.rem(z + j, zn) * 2 + c).start()
    elem_copy(me, z, partner).start()

    def use_sources(b):
        inv_copy(b).wait()
        for kind in range(CHUNKS):
            cols = pl.ds(pl.multiple_of(b * slice_len + kind * width, LANES), width)
            acc[...] += dot(stack_hi_lo(gath[kind, b]), stack_hi_lo(m32[:, cols]), NT)

    def use_records(b):
        values = jnp.concatenate([rec[b, j * STEPS : (j + 1) * STEPS, :] for j in range(peers)], axis=1)
        tag = rec[b, peers * STEPS :, :]
        owner = jnp.concatenate([tag[j : j + 1, :] for j in range(peers)], axis=1)
        spot = jnp.concatenate([tag[peers + j : peers + j + 1, :] for j in range(peers)], axis=1)
        land = jnp.where(iota((ports, peers * LANES), 0).astype(F32) == spot, 1.0, 0.0).astype(BF16)
        split = jnp.concatenate([jnp.where(owner == float(r), values, 0.0) for r in range(rows)], axis=0)
        hacc[...] += dot(stack_hi_lo(split), land, NT)

    use_records(me)
    use_sources(me)
    for k in range(CHUNKS):
        line_copy(k, partner, 2, partner).wait_recv()
    use_sources(partner)

    def consume(i):
        zb, zt, valid, onward = turn(i)

        @pl.when(valid)
        def _():
            use_sources(zb * 2 + c)
            other = zb * 2 + (1 - c)
            for kind in range(CHUNKS):
                line_copy(kind, other, 2, partner).wait_recv()
            use_sources(other)

    def ring(i, carry):
        forward(i + 2, 0)
        consume(i)
        return carry

    lax.fori_loop(0, turns - 2, ring, 0)

    def pass_on(j, carry):
        zb = lax.rem(z + j, zn)
        b = zb * 2 + c
        rec_copy(b, 0, partner).wait_recv()
        rec_copy(b, zb, partner).start()
        use_records(b)
        return carry

    lax.fori_loop(1, zn, pass_on, 0)
    for j in range(1, zn):
        zb = lax.rem(z + j, zn)
        elem_copy(zb * 2 + c, 0, partner).wait_recv()
        elem_copy(zb * 2 + c, zb, partner).start()

    def last(i, carry):
        consume(i)
        return carry

    lax.fori_loop(turns - 2, turns, last, 0)

    def take(j, carry):
        b = lax.rem(z + j, zn) * 2 + (1 - c)
        rec_copy(b, 0, partner).wait_recv()
        use_records(b)
        return carry

    lax.fori_loop(0, zn, take, 0)

    landed = hacc[: rows * STEPS, :] + hacc[rows * STEPS :, :]
    landed = jnp.concatenate([landed[r * STEPS : (r + 1) * STEPS, :] for r in range(rows)], axis=1)
    first = four_terms(acc[...] - dot(stack_hi_lo(landed), mp2[...], NT))
    mine = dot(stack_hi_lo(first), slot_own.astype(BF16))
    fst[me] = mine[:STEPS] + mine[STEPS:]
    for j in range(1, rows):
        fst_copy(me, j - 1, lax.rem(me + j, rows)).start()

    for j in range(zn):
        elem_copy(lax.rem(z + j, zn) * 2 + (1 - c), 0, partner).wait_recv()

    w = elem[...].reshape(total, total)
    self_row = jnp.sum(jnp.where(iota((total, total), 0) == iota((total, total), 1), w, 0.0), axis=0, keepdims=True)
    w_hi, w_lo = hi_lo(jnp.transpose(w))
    wc[:, :total] = w_hi
    wc[:, total:] = w_lo

    full = (8, total)
    is_arrest = iota(full, 1) % elems < arrests
    arrest_gain = jnp.where(is_arrest, jnp.broadcast_to(all_par[1:2, :], full), 0.0)
    core_gain = jnp.where(is_arrest, 0.0, jnp.broadcast_to(all_par[2:3, :], full))
    elem_self = jnp.broadcast_to(self_row, full)
    volts0 = jnp.broadcast_to(all_par[3:4, :], full)
    flux0 = jnp.broadcast_to(all_par[4:5, :], full)
    put = jnp.where(jnp.logical_and(at_slot, owner_of == me), 1.0, 0.0).astype(BF16)
    here = dot(jnp.ones((8, total), BF16), put, NT)[0:1]

    for j in range(1, subs):
        sub_copy(j).wait_send()
    for k in range(CHUNKS):
        @pl.when(z + 1 < zn)
        def _():
            line_copy(k, me, 0, partner).wait_send()

        @pl.when(z > 0)
        def _():
            line_copy(k, me, 1, partner).wait_send()

        line_copy(k, me, 2, partner).wait_send()

    def drain(i, carry):
        zb, zt, valid, onward = turn(i)
        b = zb * 2 + c

        @pl.when(valid)
        def _():
            for kind in range(CHUNKS):
                @pl.when(onward)
                def _():
                    line_copy(kind, b, 0, partner).wait_send()

                line_copy(kind, b, 2, partner).wait_send()

        return carry

    lax.fori_loop(0, turns, drain, 0)
    for j in range(1, rows):
        par_copy(me, j - 1, partner).wait_send()
    for at in range(2 * zn - 1):
        rec_copy(me, at, partner).wait_send()
        elem_copy(me, at, partner).wait_send()

    for j in range(1, rows):
        fst_copy(lax.rem(me + j, rows), j - 1, partner).wait_recv()
    fall[...] = jnp.concatenate(
        [sum(fst[h * group + i] for i in range(group)) for h in range(halves)], axis=1
    )

    def advance(t, carry):
        voltage, flux_now = carry
        first_now = jnp.broadcast_to(fall[pl.ds(t, 1), :], full)
        iterate = voltage
        for newton_pass in range(NEWTON):
            linked = flux_now + half_step * (iterate + voltage)
            ratio = iterate * (1.0 / knee_volts)
            rr = ratio * ratio
            ll = linked * linked
            current = arrest_gain * (iterate * (1.0 + rr)) + core_gain * (linked * (1.0 + cubic_term * ll))
            slope = arrest_gain * (1.0 + 3.0 * rr) + core_gain * (half_step + (half_step * 3.0 * cubic_term) * ll)
            recip = 1.0 / (1.0 + elem_self * slope)
            got = dot(stack_hi_lo(current), wc[...])
            coupled = got[:8, :total] + got[8:, :total] + got[:8, total:]
            iterate = iterate - (iterate - first_now + coupled) * recip
        vo[pl.ds(t, 1), :] = iterate[0:1]
        cu[pl.ds(t, 1), :] = current[0:1]
        return iterate, flux_now + half_step * (iterate + voltage)

    lax.fori_loop(0, STEPS, advance, (volts0, flux0))

    reach = four_terms(dot(stack_hi_lo(cu[...]), x2[...], NT))
    placed = dot(stack_hi_lo(vo[...]), put, NT)
    stacked = jnp.where(here > 0.5, placed[:STEPS] + placed[STEPS:], first - reach)
    out[:STEPS, :] = stacked
    summed = jnp.sum(stacked, axis=0, keepdims=True)
    last_flux = flux[...] + half_step * (prev[...] + 2.0 * summed - stacked[STEPS - 1 : STEPS])
    out[STEPS:, :] = jnp.broadcast_to(last_flux, (8, ports))
    for j in range(1, rows):
        fst_copy(me, j - 1, partner).wait_send()


def on_device(subs, rows, *args):
    inverse, sources = args[0], args[1]
    ports = inverse.shape[1]
    order = inverse.shape[2]
    slice_len = sources.shape[2]
    arrests, cores = args[10].shape[1], args[11].shape[1]
    elems = arrests + cores
    total = rows * elems
    zn = rows // 2
    tag_rows = -(-2 * (subs - 1) // 8) * 8
    vmem = pl.BlockSpec(memory_space=pltpu.VMEM)
    hbm = pl.BlockSpec(memory_space=pl.ANY)
    dma = pltpu.SemaphoreType.DMA
    small = args[2:]
    both = pl.pallas_call(
        functools.partial(kernel, subs, rows, ports, slice_len, arrests, cores, len(small)),
        out_shape=jax.ShapeDtypeStruct((STEPS + 8, ports), F32),
        in_specs=[hbm] * len(args),
        out_specs=vmem,
        scratch_shapes=[pltpu.VMEM(a.shape, a.dtype) for a in small]
        + [
            pltpu.VMEM((ports, order), F32),
            pltpu.VMEM((ports, rows * ports), F32),
            pltpu.VMEM((2 * ports, rows * ports), BF16),
            pltpu.VMEM((CHUNKS, rows, STEPS, slice_len // CHUNKS), F32),
            pltpu.VMEM((subs - 1, STEPS + 8, LANES), F32),
            pltpu.VMEM((rows, (subs - 1) * STEPS + tag_rows, LANES), F32),
            pltpu.VMEM((rows, elems, total), F32),
            pltpu.VMEM((rows, 8, LANES), F32),
            pltpu.VMEM((rows, STEPS, LANES), F32),
            pltpu.VMEM((STEPS + 8, LANES), F32),
            pltpu.VMEM((2 * ports, total), BF16),
            pltpu.VMEM((total, 2 * total), BF16),
            pltpu.VMEM((STEPS, total), F32),
            pltpu.VMEM((STEPS, total), F32),
            pltpu.VMEM((STEPS, total), F32),
            pltpu.VMEM((2 * STEPS, 2 * ports), F32),
            pltpu.VMEM((2 * STEPS * rows, ports), F32),
            dma((len(small),)),
            dma((rows,)),
            dma((rows,)),
            dma((CHUNKS,)),
            dma((CHUNKS, rows, 3)),
            dma((CHUNKS, rows)),
            dma((subs - 1,)),
            dma((subs - 1,)),
            dma((2 * zn - 1,)),
            dma((rows,)),
            dma((rows - 1,)),
            dma((rows,)),
            dma((2 * zn - 1,)),
            dma((rows,)),
            dma((rows - 1,)),
            dma((rows,)),
        ],
        compiler_params=pltpu.CompilerParams(collective_id=0, has_side_effects=True),
        name="window",
    )(*args)
    return both[None, :STEPS], both[STEPS : STEPS + 1]


def solution(mesh):
    subs, rows = mesh.shape["sub"], mesh.shape["row"]
    in_specs = (
        P("sub", "row", None),
        P("sub", None, "row"),
        P("sub", None, "row"),
    ) + (P("sub", "row"),) * 9
    out_specs = (P("sub", None, "row"), P("sub", "row"))
    return jax.shard_map(
        functools.partial(on_device, subs, rows),
        mesh=mesh, in_specs=in_specs, out_specs=out_specs, check_vma=False,
    )
```

```python
import functools

import jax
import jax.numpy as jnp
from jax import lax
from jax.experimental import pallas as pl
from jax.experimental.pallas import tpu as pltpu
from jax.sharding import PartitionSpec as P

STEPS = 16
HISTORY = 32
NEWTON = 2
CHUNKS = 2
LANES = 128

half_step = 0.25
knee_volts = 1.5
cubic_term = 0.25

F32 = jnp.float32
BF16 = jnp.bfloat16
MESH = pl.DeviceIdType.MESH
NN = (((1,), (0,)), ((), ()))
NT = (((1,), (1,)), ((), ()))
HIGHEST = lax.Precision.HIGHEST


def iota(shape, axis):
    return lax.broadcasted_iota(jnp.int32, shape, axis)


def hi_lo(x):
    high = x.astype(BF16)
    return high, (x - high.astype(F32)).astype(BF16)


def stack_hi_lo(x):
    return jnp.concatenate(hi_lo(x), axis=0)


def dot(a, b, dims=NN):
    return lax.dot_general(a, b, dims, preferred_element_type=F32)


def four_terms(r):
    n, m = r.shape[0] // 2, r.shape[1] // 2
    return (r[:n, :m] + r[n:, :m]) + (r[:n, m:] + r[n:, m:])


def kernel(
    subs, rows, ports, slice_len, arrests, cores, n_small,
    inv, src, *refs,
):
    small_hbm, refs = refs[:n_small], refs[n_small:]
    out, refs = refs[0], refs[1:]
    small, refs = refs[:n_small], refs[n_small:]
    (
        m32, m2, mp32, mp2, gath, recin, rec, elem, par, fst, recout, x2, wc, fall, vo, cu, acc, hacc,
        small_sem, inv_sem, mp_sem, src_sem, line_send, line_recv, sub_send, sub_recv,
        rec_send, rec_recv, par_send, par_recv, elem_send, elem_recv, fst_send, fst_recv,
    ) = refs
    hist, dest, port, delay, prev, flux, again, cgain, aslots, cslots = small
    s = lax.axis_index("sub")
    me = lax.axis_index("row")
    z, c = me // 2, me % 2
    zn = rows // 2
    partner = z * 2 + (1 - c)
    elems = arrests + cores
    group = LANES // elems
    total = rows * elems
    halves = total // LANES
    width = slice_len // CHUNKS
    peers = subs - 1
    turns = 2 * (zn - 1)

    barrier = pltpu.get_barrier_semaphore()
    for j in range(1, rows):
        pl.semaphore_signal(barrier, inc=1, device_id=(s, lax.rem(me + j, rows)), device_id_type=MESH)
    for j in range(1, subs):
        pl.semaphore_signal(barrier, inc=1, device_id=(lax.rem(s + j, subs), me), device_id_type=MESH)

    small_copies = [
        pltpu.make_async_copy(small_hbm[i], small[i], small_sem.at[i]) for i in range(n_small)
    ]
    for copy in small_copies:
        copy.start()

    def src_copy(k):
        return pltpu.make_async_copy(
            src.at[0, :, pl.ds(k * width, width)], gath.at[k, me], src_sem.at[k]
        )

    for k in range(CHUNKS):
        src_copy(k).start()

    def mp_copy(r):
        return pltpu.make_async_copy(
            inv.at[0, :, pl.ds(r * slice_len, ports)], mp32.at[:, pl.ds(r * ports, ports)], mp_sem.at[r]
        )

    for r in range(rows):
        mp_copy(r).start()

    def inv_copy(b):
        cols = pl.ds(pl.multiple_of(b * slice_len, LANES), slice_len)
        return pltpu.make_async_copy(inv.at[0, :, cols], m32.at[:, cols], inv_sem.at[b])

    steps_z = [0]
    for j in range(1, zn):
        hop = (j + 1) // 2
        steps_z.append(hop if j % 2 == 1 else zn - hop)
    for hop in steps_z:
        zb = lax.rem(z + hop, zn)
        inv_copy(zb * 2 + c).start()
        inv_copy(zb * 2 + (1 - c)).start()

    for copy in small_copies:
        copy.wait()

    shifted = hist[0]
    shift = HISTORY - delay[...]
    bit = 1
    while bit <= HISTORY - STEPS:
        moved = pltpu.roll(shifted, HISTORY - bit, 0)
        shifted = jnp.where((shift // bit) % 2 == 1, moved, shifted)
        bit *= 2
    recout[:STEPS, :] = shifted[:STEPS, :]
    k8 = iota((8, LANES), 0)
    tags = jnp.where(k8 == 0, dest[...], jnp.where(k8 == 1, port[...] // ports, port[...] % ports))
    recout[STEPS:, :] = tags.astype(F32)

    lane16a, row16a = iota((arrests, LANES), 1), iota((arrests, LANES), 0)
    lane16c, row16c = iota((cores, LANES), 1), iota((cores, LANES), 0)
    put_a = jnp.where(lane16a % elems == row16a, 1.0, 0.0).astype(BF16)
    put_c = jnp.where(lane16c % elems == row16c + arrests, 1.0, 0.0).astype(BF16)
    slot_a = jnp.broadcast_to(aslots[...].astype(F32), (8, arrests)).astype(BF16)
    slot_c = jnp.broadcast_to(cslots[...].astype(F32), (8, cores)).astype(BF16)
    slot_row = (dot(slot_a, put_a) + dot(slot_c, put_c))[0:1, :]
    hit = iota((ports, LANES), 0).astype(F32) == slot_row
    slot_tiled = jnp.where(hit, 1.0, 0.0)
    slot_own = jnp.where(iota((ports, LANES), 1) // elems == me % group, slot_tiled, 0.0)
    r8 = iota((8, ports), 0)
    params = jnp.where(
        r8 == 0,
        iota((8, ports), 1).astype(F32),
        jnp.where(
            r8 == 1,
            again[...],
            jnp.where(r8 == 2, cgain[...], jnp.where(r8 == 3, prev[...], flux[...])),
        ),
    )
    par[me] = lax.dot_general(params, slot_own, NN, precision=HIGHEST, preferred_element_type=F32)

    for r in range(rows):
        mp_copy(r).wait()
    mp_hi, mp_lo = hi_lo(mp32[...])
    mp2[:ports, :] = mp_hi
    mp2[ports:, :] = mp_lo
    acc[...] = jnp.zeros_like(acc)
    hacc[...] = jnp.zeros_like(hacc)

    def split_block(j, carry):
        b = lax.rem(me + j, rows)
        inv_copy(b).wait()
        cols = pl.ds(pl.multiple_of(b * slice_len, LANES), slice_len)
        high, low = hi_lo(m32[:, cols])
        m2[:ports, cols] = high
        m2[ports:, cols] = low
        return carry

    def use_sources(b):
        for kind in range(CHUNKS):
            cols = pl.ds(pl.multiple_of(b * slice_len + kind * width, LANES), width)
            acc[...] += dot(stack_hi_lo(gath[kind, b]), m2[:, cols], NT)

    lax.fori_loop(0, rows, split_block, 0)
    for k in range(CHUNKS):
        src_copy(k).wait()
    use_sources(me)
    pl.semaphore_wait(barrier, rows + subs - 2)

    def remote(ref_from, ref_to, send, recv, to_sub, to_row):
        return pltpu.make_async_remote_copy(
            src_ref=ref_from, dst_ref=ref_to, send_sem=send, recv_sem=recv,
            device_id=(to_sub, to_row), device_id_type=MESH,
        )

    def sub_copy(j):
        return remote(
            recout, recin.at[peers - j], sub_send.at[j - 1], sub_recv.at[peers - j],
            lax.rem(s + j, subs), me,
        )

    def par_copy(b, at, target):
        return remote(par.at[b], par.at[b], par_send.at[at], par_recv.at[b], s, target)

    def line_copy(kind, b, way, target):
        ref = gath.at[kind, b]
        return remote(ref, ref, line_send.at[kind, b, way], line_recv.at[kind, b], s, target)

    def rec_copy(b, at, target):
        return remote(rec.at[b], rec.at[b], rec_send.at[at], rec_recv.at[b], s, target)

    def elem_copy(b, at, target):
        return remote(elem.at[b], elem.at[b], elem_send.at[at], elem_recv.at[b], s, target)

    def fst_copy(b, at, target):
        return remote(fst.at[b], fst.at[b], fst_send.at[at], fst_recv.at[b], s, target)

    for j in range(1, subs):
        sub_copy(j).start()
    for j in range(1, rows):
        par_copy(me, j - 1, lax.rem(me + j, rows)).start()
    for k in range(CHUNKS):
        @pl.when(z + 1 < zn)
        def _():
            line_copy(k, me, 0, me + 2).start()

        @pl.when(z > 0)
        def _():
            line_copy(k, me, 1, me - 2).start()

        line_copy(k, me, 2, partner).start()

    for j in range(1, subs):
        sub_copy(j).wait_recv()
    for j in range(peers):
        rec[me, j * STEPS : (j + 1) * STEPS, :] = recin[j, :STEPS, :]
    named = [
        jnp.where(
            recin[j, STEPS : STEPS + 1, :] == s.astype(F32), recin[j, STEPS + 1 : STEPS + 2, :], -1.0
        )
        for j in range(peers)
    ]
    spots = [recin[j, STEPS + 2 : STEPS + 3, :] for j in range(peers)]
    for j, row in enumerate(named + spots):
        rec[me, peers * STEPS + j : peers * STEPS + j + 1, :] = row
    for j in range(1, zn):
        rec_copy(me, zn + j - 1, lax.rem(z + j, zn) * 2 + c).start()
    rec_copy(me, z, partner).start()

    def turn(i):
        below = i % 2 == 0
        k = i // 2 + 1
        zb = jnp.where(below, z - k, z + k)
        zt = jnp.where(below, z + 1, z - 1)
        return zb, zt, jnp.logical_and(zb >= 0, zb < zn), jnp.logical_and(zt >= 0, zt < zn)

    def forward(i, carry):
        zb, zt, valid, onward = turn(i)
        b = zb * 2 + c

        @pl.when(valid)
        def _():
            for kind in range(CHUNKS):
                line_copy(kind, b, 0, partner).wait_recv()

                @pl.when(onward)
                def _():
                    line_copy(kind, b, 0, zt * 2 + c).start()

                line_copy(kind, b, 2, partner).start()

        return carry

    lax.fori_loop(0, 2, forward, 0)

    def use_records(b):
        values = jnp.concatenate([rec[b, j * STEPS : (j + 1) * STEPS, :] for j in range(peers)], axis=1)
        tag = rec[b, peers * STEPS :, :]
        owner = jnp.concatenate([tag[j : j + 1, :] for j in range(peers)], axis=1)
        spot = jnp.concatenate([tag[peers + j : peers + j + 1, :] for j in range(peers)], axis=1)
        land = jnp.where(iota((ports, peers * LANES), 0).astype(F32) == spot, 1.0, 0.0).astype(BF16)
        split = jnp.concatenate([jnp.where(owner == float(r), values, 0.0) for r in range(rows)], axis=0)
        hacc[...] += dot(stack_hi_lo(split), land, NT)

    use_records(me)
    for k in range(CHUNKS):
        line_copy(k, partner, 2, partner).wait_recv()
    use_sources(partner)

    def consume(i):
        zb, zt, valid, onward = turn(i)

        @pl.when(valid)
        def _():
            use_sources(zb * 2 + c)
            other = zb * 2 + (1 - c)
            for kind in range(CHUNKS):
                line_copy(kind, other, 2, partner).wait_recv()
            use_sources(other)

    def ring(i, carry):
        forward(i + 2, 0)
        consume(i)
        return carry

    early = min(2, turns - 2)
    lax.fori_loop(0, early, ring, 0)

    for j in range(1, rows):
        par_copy(lax.rem(me + j, rows), j - 1, partner).wait_recv()
    all_par = jnp.concatenate(
        [sum(par[h * group + i] for i in range(group)) for h in range(halves)], axis=1
    )
    slots_all = all_par[0:1, :]
    at_slot = iota((ports, total), 0).astype(F32) == slots_all
    owner_of = iota((ports, total), 1) // elems
    pick = None
    for r in range(rows):
        choose = jnp.where(jnp.logical_and(at_slot, owner_of == r), 1.0, 0.0).astype(BF16)
        term = dot(mp2[:, r * ports : (r + 1) * ports], choose)
        pick = term if pick is None else pick + term
    x2[...] = pick.astype(BF16)
    slot_cols = jnp.transpose(slot_tiled)[:elems].astype(BF16)
    elem[me] = dot(slot_cols, x2[:ports, :]) + dot(slot_cols, x2[ports:, :])
    for j in range(1, zn):
        elem_copy(me, zn + j - 1, lax.rem(z + j, zn) * 2 + c).start()
    elem_copy(me, z, partner).start()

    lax.fori_loop(early, turns - 2, ring, 0)

    def pass_on(j, carry):
        zb = lax.rem(z + j, zn)
        b = zb * 2 + c
        rec_copy(b, 0, partner).wait_recv()
        rec_copy(b, zb, partner).start()
        use_records(b)
        return carry

    lax.fori_loop(1, zn, pass_on, 0)

    def take(j, carry):
        b = lax.rem(z + j, zn) * 2 + (1 - c)
        rec_copy(b, 0, partner).wait_recv()
        use_records(b)
        return carry

    lax.fori_loop(0, zn, take, 0)

    def last(i, carry):
        consume(i)
        return carry

    lax.fori_loop(turns - 2, turns, last, 0)

    landed = hacc[: rows * STEPS, :] + hacc[rows * STEPS :, :]
    landed = jnp.concatenate([landed[r * STEPS : (r + 1) * STEPS, :] for r in range(rows)], axis=1)
    first = four_terms(acc[...] - dot(stack_hi_lo(landed), mp2[...], NT))
    mine = dot(stack_hi_lo(first), slot_own.astype(BF16))
    fst[me] = mine[:STEPS] + mine[STEPS:]
    for j in range(1, rows):
        fst_copy(me, j - 1, lax.rem(me + j, rows)).start()

    for j in range(1, zn):
        zb = lax.rem(z + j, zn)
        elem_copy(zb * 2 + c, 0, partner).wait_recv()
        elem_copy(zb * 2 + c, zb, partner).start()
    for j in range(zn):
        elem_copy(lax.rem(z + j, zn) * 2 + (1 - c), 0, partner).wait_recv()

    w = elem[...].reshape(total, total)
    self_row = jnp.sum(jnp.where(iota((total, total), 0) == iota((total, total), 1), w, 0.0), axis=0, keepdims=True)
    w_hi, w_lo = hi_lo(jnp.transpose(w))
    wc[:, :total] = w_hi
    wc[:, total:] = w_lo

    full = (8, total)
    is_arrest = iota(full, 1) % elems < arrests
    arrest_gain = jnp.where(is_arrest, jnp.broadcast_to(all_par[1:2, :], full), 0.0)
    core_gain = jnp.where(is_arrest, 0.0, jnp.broadcast_to(all_par[2:3, :], full))
    elem_self = jnp.broadcast_to(self_row, full)
    volts0 = jnp.broadcast_to(all_par[3:4, :], full)
    flux0 = jnp.broadcast_to(all_par[4:5, :], full)
    put = jnp.where(jnp.logical_and(at_slot, owner_of == me), 1.0, 0.0).astype(BF16)
    here = dot(jnp.ones((8, total), BF16), put, NT)[0:1]

    for j in range(1, subs):
        sub_copy(j).wait_send()
    for k in range(CHUNKS):
        @pl.when(z + 1 < zn)
        def _():
            line_copy(k, me, 0, partner).wait_send()

        @pl.when(z > 0)
        def _():
            line_copy(k, me, 1, partner).wait_send()

        line_copy(k, me, 2, partner).wait_send()

    def drain(i, carry):
        zb, zt, valid, onward = turn(i)
        b = zb * 2 + c

        @pl.when(valid)
        def _():
            for kind in range(CHUNKS):
                @pl.when(onward)
                def _():
                    line_copy(kind, b, 0, partner).wait_send()

                line_copy(kind, b, 2, partner).wait_send()

        return carry

    lax.fori_loop(0, turns, drain, 0)
    for j in range(1, rows):
        par_copy(me, j - 1, partner).wait_send()
    for at in range(2 * zn - 1):
        rec_copy(me, at, partner).wait_send()
        elem_copy(me, at, partner).wait_send()

    for j in range(1, rows):
        fst_copy(lax.rem(me + j, rows), j - 1, partner).wait_recv()
    fall[...] = jnp.concatenate(
        [sum(fst[h * group + i] for i in range(group)) for h in range(halves)], axis=1
    )

    def advance(t, carry):
        voltage, flux_now = carry
        first_now = jnp.broadcast_to(fall[pl.ds(t, 1), :], full)
        iterate = voltage
        for newton_pass in range(NEWTON):
            linked = flux_now + half_step * (iterate + voltage)
            ratio = iterate * (1.0 / knee_volts)
            rr = ratio * ratio
            ll = linked * linked
            current = arrest_gain * (iterate * (1.0 + rr)) + core_gain * (linked * (1.0 + cubic_term * ll))
            slope = arrest_gain * (1.0 + 3.0 * rr) + core_gain * (half_step + (half_step * 3.0 * cubic_term) * ll)
            recip = 1.0 / (1.0 + elem_self * slope)
            got = dot(stack_hi_lo(current), wc[...])
            coupled = got[:8, :total] + got[8:, :total] + got[:8, total:]
            iterate = iterate - (iterate - first_now + coupled) * recip
        vo[pl.ds(t, 1), :] = iterate[0:1]
        cu[pl.ds(t, 1), :] = current[0:1]
        return iterate, flux_now + half_step * (iterate + voltage)

    lax.fori_loop(0, STEPS, advance, (volts0, flux0))

    reach = four_terms(dot(stack_hi_lo(cu[...]), x2[...], NT))
    placed = dot(stack_hi_lo(vo[...]), put, NT)
    stacked = jnp.where(here > 0.5, placed[:STEPS] + placed[STEPS:], first - reach)
    out[:STEPS, :] = stacked
    summed = jnp.sum(stacked, axis=0, keepdims=True)
    last_flux = flux[...] + half_step * (prev[...] + 2.0 * summed - stacked[STEPS - 1 : STEPS])
    out[STEPS:, :] = jnp.broadcast_to(last_flux, (8, ports))
    for j in range(1, rows):
        fst_copy(me, j - 1, partner).wait_send()


def give(both, volts, last_flux):
    volts[0] = both[:STEPS, :]
    last_flux[...] = both[STEPS : STEPS + 1, :]


def on_device(subs, rows, *args):
    inverse, sources = args[0], args[1]
    ports = inverse.shape[1]
    order = inverse.shape[2]
    slice_len = sources.shape[2]
    arrests, cores = args[10].shape[1], args[11].shape[1]
    elems = arrests + cores
    total = rows * elems
    zn = rows // 2
    tag_rows = -(-2 * (subs - 1) // 8) * 8
    vmem = pl.BlockSpec(memory_space=pltpu.VMEM)
    hbm = pl.BlockSpec(memory_space=pl.ANY)
    dma = pltpu.SemaphoreType.DMA
    small = args[2:]
    both = pl.pallas_call(
        functools.partial(kernel, subs, rows, ports, slice_len, arrests, cores, len(small)),
        out_shape=jax.ShapeDtypeStruct((STEPS + 8, ports), F32),
        in_specs=[hbm] * len(args),
        out_specs=vmem,
        scratch_shapes=[pltpu.VMEM(a.shape, a.dtype) for a in small]
        + [
            pltpu.VMEM((ports, order), F32),
            pltpu.VMEM((2 * ports, order), BF16),
            pltpu.VMEM((ports, rows * ports), F32),
            pltpu.VMEM((2 * ports, rows * ports), BF16),
            pltpu.VMEM((CHUNKS, rows, STEPS, slice_len // CHUNKS), F32),
            pltpu.VMEM((subs - 1, STEPS + 8, LANES), F32),
            pltpu.VMEM((rows, (subs - 1) * STEPS + tag_rows, LANES), F32),
            pltpu.VMEM((rows, elems, total), F32),
            pltpu.VMEM((rows, 8, LANES), F32),
            pltpu.VMEM((rows, STEPS, LANES), F32),
            pltpu.VMEM((STEPS + 8, LANES), F32),
            pltpu.VMEM((2 * ports, total), BF16),
            pltpu.VMEM((total, 2 * total), BF16),
            pltpu.VMEM((STEPS, total), F32),
            pltpu.VMEM((STEPS, total), F32),
            pltpu.VMEM((STEPS, total), F32),
            pltpu.VMEM((2 * STEPS, 2 * ports), F32),
            pltpu.VMEM((2 * STEPS * rows, ports), F32),
            dma((len(small),)),
            dma((rows,)),
            dma((rows,)),
            dma((CHUNKS,)),
            dma((CHUNKS, rows, 3)),
            dma((CHUNKS, rows)),
            dma((subs - 1,)),
            dma((subs - 1,)),
            dma((2 * zn - 1,)),
            dma((rows,)),
            dma((rows - 1,)),
            dma((rows,)),
            dma((2 * zn - 1,)),
            dma((rows,)),
            dma((rows - 1,)),
            dma((rows,)),
        ],
        compiler_params=pltpu.CompilerParams(collective_id=0, has_side_effects=True),
        name="window",
    )(*args)
    return pl.pallas_call(
        give,
        out_shape=(
            jax.ShapeDtypeStruct((1, STEPS, ports), F32),
            jax.ShapeDtypeStruct((1, ports), F32),
        ),
        in_specs=[vmem],
        out_specs=(vmem, vmem),
        name="give",
    )(both)


def solution(mesh):
    subs, rows = mesh.shape["sub"], mesh.shape["row"]
    in_specs = (
        P("sub", "row", None),
        P("sub", None, "row"),
        P("sub", None, "row"),
    ) + (P("sub", "row"),) * 9
    out_specs = (P("sub", None, "row"), P("sub", "row"))
    return jax.shard_map(
        functools.partial(on_device, subs, rows),
        mesh=mesh, in_specs=in_specs, out_specs=out_specs, check_vma=False,
    )
```

```python
import functools

import jax
import jax.numpy as jnp
from jax import lax
from jax.experimental import pallas as pl
from jax.experimental.pallas import tpu as pltpu
from jax.sharding import PartitionSpec as P

STEPS = 16
HISTORY = 32
NEWTON = 2
CHUNKS = 2
LANES = 128

half_step = 0.25
knee_volts = 1.5
cubic_term = 0.25

F32 = jnp.float32
BF16 = jnp.bfloat16
MESH = pl.DeviceIdType.MESH
NN = (((1,), (0,)), ((), ()))
NT = (((1,), (1,)), ((), ()))
HIGHEST = lax.Precision.HIGHEST


def iota(shape, axis):
    return lax.broadcasted_iota(jnp.int32, shape, axis)


def hi_lo(x):
    high = x.astype(BF16)
    return high, (x - high.astype(F32)).astype(BF16)


def stack_hi_lo(x):
    return jnp.concatenate(hi_lo(x), axis=0)


def dot(a, b, dims=NN):
    return lax.dot_general(a, b, dims, preferred_element_type=F32)


def four_terms(r):
    n, m = r.shape[0] // 2, r.shape[1] // 2
    return (r[:n, :m] + r[n:, :m]) + (r[:n, m:] + r[n:, m:])


def kernel(
    subs, rows, ports, slice_len, arrests, cores, n_small,
    inv, src, *refs,
):
    small_hbm, refs = refs[:n_small], refs[n_small:]
    out, refs = refs[0], refs[1:]
    small, refs = refs[:n_small], refs[n_small:]
    (
        m32, m2, mp32, mp2, gath, recin, rec, elem, par, fst, recout, x2, wc, fall, vo, cu, acc, hacc,
        small_sem, inv_sem, mp_sem, src_sem, line_send, line_recv, sub_send, sub_recv,
        rec_send, rec_recv, par_send, par_recv, elem_send, elem_recv, fst_send, fst_recv,
    ) = refs
    hist, dest, port, delay, prev, flux, again, cgain, aslots, cslots = small
    s = lax.axis_index("sub")
    me = lax.axis_index("row")
    z, c = me // 2, me % 2
    zn = rows // 2
    partner = z * 2 + (1 - c)
    elems = arrests + cores
    group = LANES // elems
    total = rows * elems
    halves = total // LANES
    width = slice_len // CHUNKS
    peers = subs - 1
    turns = 2 * (zn - 1)

    barrier = pltpu.get_barrier_semaphore()
    for j in range(1, rows):
        pl.semaphore_signal(barrier, inc=1, device_id=(s, lax.rem(me + j, rows)), device_id_type=MESH)
    for j in range(1, subs):
        pl.semaphore_signal(barrier, inc=1, device_id=(lax.rem(s + j, subs), me), device_id_type=MESH)

    small_copies = [
        pltpu.make_async_copy(small_hbm[i], small[i], small_sem.at[i]) for i in range(n_small)
    ]
    for copy in small_copies:
        copy.start()

    def src_copy(k):
        return pltpu.make_async_copy(
            src.at[0, :, pl.ds(k * width, width)], gath.at[k, me], src_sem.at[k]
        )

    for k in range(CHUNKS):
        src_copy(k).start()

    def mp_copy(r):
        return pltpu.make_async_copy(
            inv.at[0, :, pl.ds(r * slice_len, ports)], mp32.at[:, pl.ds(r * ports, ports)], mp_sem.at[r]
        )

    for r in range(rows):
        mp_copy(r).start()

    def inv_copy(b):
        cols = pl.ds(pl.multiple_of(b * slice_len, LANES), slice_len)
        return pltpu.make_async_copy(inv.at[0, :, cols], m32.at[:, cols], inv_sem.at[b])

    steps_z = [0]
    for j in range(1, zn):
        hop = (j + 1) // 2
        steps_z.append(hop if j % 2 == 1 else zn - hop)
    for hop in steps_z:
        zb = lax.rem(z + hop, zn)
        inv_copy(zb * 2 + c).start()
        inv_copy(zb * 2 + (1 - c)).start()

    for copy in small_copies:
        copy.wait()

    shifted = hist[0]
    shift = HISTORY - delay[...]
    bit = 1
    while bit <= HISTORY - STEPS:
        moved = pltpu.roll(shifted, HISTORY - bit, 0)
        shifted = jnp.where((shift // bit) % 2 == 1, moved, shifted)
        bit *= 2
    recout[:STEPS, :] = shifted[:STEPS, :]
    k8 = iota((8, LANES), 0)
    tags = jnp.where(k8 == 0, dest[...], jnp.where(k8 == 1, port[...] // ports, port[...] % ports))
    recout[STEPS:, :] = tags.astype(F32)

    lane16a, row16a = iota((arrests, LANES), 1), iota((arrests, LANES), 0)
    lane16c, row16c = iota((cores, LANES), 1), iota((cores, LANES), 0)
    put_a = jnp.where(lane16a % elems == row16a, 1.0, 0.0).astype(BF16)
    put_c = jnp.where(lane16c % elems == row16c + arrests, 1.0, 0.0).astype(BF16)
    slot_a = jnp.broadcast_to(aslots[...].astype(F32), (8, arrests)).astype(BF16)
    slot_c = jnp.broadcast_to(cslots[...].astype(F32), (8, cores)).astype(BF16)
    slot_row = (dot(slot_a, put_a) + dot(slot_c, put_c))[0:1, :]
    hit = iota((ports, LANES), 0).astype(F32) == slot_row
    slot_tiled = jnp.where(hit, 1.0, 0.0)
    slot_own = jnp.where(iota((ports, LANES), 1) // elems == me % group, slot_tiled, 0.0)
    r8 = iota((8, ports), 0)
    params = jnp.where(
        r8 == 0,
        iota((8, ports), 1).astype(F32),
        jnp.where(
            r8 == 1,
            again[...],
            jnp.where(r8 == 2, cgain[...], jnp.where(r8 == 3, prev[...], flux[...])),
        ),
    )
    par[me] = lax.dot_general(params, slot_own, NN, precision=HIGHEST, preferred_element_type=F32)

    for r in range(rows):
        mp_copy(r).wait()
    mp_hi, mp_lo = hi_lo(mp32[...])
    mp2[:ports, :] = mp_hi
    mp2[ports:, :] = mp_lo
    acc[...] = jnp.zeros_like(acc)
    hacc[...] = jnp.zeros_like(hacc)

    def split_block(j, carry):
        b = lax.rem(me + j, rows)
        inv_copy(b).wait()
        cols = pl.ds(pl.multiple_of(b * slice_len, LANES), slice_len)
        high, low = hi_lo(m32[:, cols])
        m2[:ports, cols] = high
        m2[ports:, cols] = low
        return carry

    def use_sources(b):
        for kind in range(CHUNKS):
            cols = pl.ds(pl.multiple_of(b * slice_len + kind * width, LANES), width)
            acc[...] += dot(stack_hi_lo(gath[kind, b]), m2[:, cols], NT)

    lax.fori_loop(0, rows, split_block, 0)
    for k in range(CHUNKS):
        src_copy(k).wait()
    use_sources(me)
    pl.semaphore_wait(barrier, rows + subs - 2)

    def remote(ref_from, ref_to, send, recv, to_sub, to_row):
        return pltpu.make_async_remote_copy(
            src_ref=ref_from, dst_ref=ref_to, send_sem=send, recv_sem=recv,
            device_id=(to_sub, to_row), device_id_type=MESH,
        )

    def sub_copy(j):
        return remote(
            recout, recin.at[peers - j], sub_send.at[j - 1], sub_recv.at[peers - j],
            lax.rem(s + j, subs), me,
        )

    def par_copy(b, at, target):
        return remote(par.at[b], par.at[b], par_send.at[at], par_recv.at[b], s, target)

    def line_copy(kind, b, way, target):
        ref = gath.at[kind, b]
        return remote(ref, ref, line_send.at[kind, b, way], line_recv.at[kind, b], s, target)

    def rec_copy(b, at, target):
        return remote(rec.at[b], rec.at[b], rec_send.at[at], rec_recv.at[b], s, target)

    def elem_copy(b, at, target):
        return remote(elem.at[b], elem.at[b], elem_send.at[at], elem_recv.at[b], s, target)

    def fst_copy(b, at, target):
        return remote(fst.at[b], fst.at[b], fst_send.at[at], fst_recv.at[b], s, target)

    for j in range(1, subs):
        sub_copy(j).start()
    for j in range(1, rows):
        par_copy(me, j - 1, lax.rem(me + j, rows)).start()
    for k in range(CHUNKS):
        @pl.when(z + 1 < zn)
        def _():
            line_copy(k, me, 0, me + 2).start()

        @pl.when(z > 0)
        def _():
            line_copy(k, me, 1, me - 2).start()

        line_copy(k, me, 2, partner).start()

    for j in range(1, subs):
        sub_copy(j).wait_recv()
    for j in range(peers):
        rec[me, j * STEPS : (j + 1) * STEPS, :] = recin[j, :STEPS, :]
    named = [
        jnp.where(
            recin[j, STEPS : STEPS + 1, :] == s.astype(F32), recin[j, STEPS + 1 : STEPS + 2, :], -1.0
        )
        for j in range(peers)
    ]
    spots = [recin[j, STEPS + 2 : STEPS + 3, :] for j in range(peers)]
    for j, row in enumerate(named + spots):
        rec[me, peers * STEPS + j : peers * STEPS + j + 1, :] = row
    for j in range(1, zn):
        rec_copy(me, zn + j - 1, lax.rem(z + j, zn) * 2 + c).start()
    rec_copy(me, z, partner).start()

    def turn(i):
        below = i % 2 == 0
        k = i // 2 + 1
        zb = jnp.where(below, z - k, z + k)
        zt = jnp.where(below, z + 1, z - 1)
        return zb, zt, jnp.logical_and(zb >= 0, zb < zn), jnp.logical_and(zt >= 0, zt < zn)

    def forward(i, carry):
        zb, zt, valid, onward = turn(i)
        b = zb * 2 + c

        @pl.when(valid)
        def _():
            for kind in range(CHUNKS):
                line_copy(kind, b, 0, partner).wait_recv()

                @pl.when(onward)
                def _():
                    line_copy(kind, b, 0, zt * 2 + c).start()

                line_copy(kind, b, 2, partner).start()

        return carry

    lax.fori_loop(0, 2, forward, 0)

    def use_records(b):
        values = jnp.concatenate([rec[b, j * STEPS : (j + 1) * STEPS, :] for j in range(peers)], axis=1)
        tag = rec[b, peers * STEPS :, :]
        owner = jnp.concatenate([tag[j : j + 1, :] for j in range(peers)], axis=1)
        spot = jnp.concatenate([tag[peers + j : peers + j + 1, :] for j in range(peers)], axis=1)
        land = jnp.where(iota((ports, peers * LANES), 0).astype(F32) == spot, 1.0, 0.0).astype(BF16)
        split = jnp.concatenate([jnp.where(owner == float(r), values, 0.0) for r in range(rows)], axis=0)
        hacc[...] += dot(stack_hi_lo(split), land, NT)

    use_records(me)
    for k in range(CHUNKS):
        line_copy(k, partner, 2, partner).wait_recv()
    use_sources(partner)

    def consume(i):
        zb, zt, valid, onward = turn(i)

        @pl.when(valid)
        def _():
            use_sources(zb * 2 + c)
            other = zb * 2 + (1 - c)
            for kind in range(CHUNKS):
                line_copy(kind, other, 2, partner).wait_recv()
            use_sources(other)

    def ring(i, carry):
        forward(i + 2, 0)
        consume(i)
        return carry

    early = min(2, turns - 2)
    lax.fori_loop(0, early, ring, 0)

    for j in range(1, rows):
        par_copy(lax.rem(me + j, rows), j - 1, partner).wait_recv()
    all_par = jnp.concatenate(
        [sum(par[h * group + i] for i in range(group)) for h in range(halves)], axis=1
    )
    slots_all = all_par[0:1, :]
    at_slot = iota((ports, total), 0).astype(F32) == slots_all
    owner_of = iota((ports, total), 1) // elems
    pick = None
    for r in range(rows):
        choose = jnp.where(jnp.logical_and(at_slot, owner_of == r), 1.0, 0.0).astype(BF16)
        term = dot(mp2[:, r * ports : (r + 1) * ports], choose)
        pick = term if pick is None else pick + term
    x2[...] = pick.astype(BF16)
    slot_cols = jnp.transpose(slot_tiled)[:elems].astype(BF16)
    elem[me] = dot(slot_cols, x2[:ports, :]) + dot(slot_cols, x2[ports:, :])
    for j in range(1, zn):
        elem_copy(me, zn + j - 1, lax.rem(z + j, zn) * 2 + c).start()
    elem_copy(me, z, partner).start()

    lax.fori_loop(early, turns - 2, ring, 0)

    def pass_on(j, carry):
        zb = lax.rem(z + j, zn)
        b = zb * 2 + c
        rec_copy(b, 0, partner).wait_recv()
        rec_copy(b, zb, partner).start()
        use_records(b)
        return carry

    lax.fori_loop(1, zn, pass_on, 0)

    def take(j, carry):
        b = lax.rem(z + j, zn) * 2 + (1 - c)
        rec_copy(b, 0, partner).wait_recv()
        use_records(b)
        return carry

    lax.fori_loop(0, zn, take, 0)

    def last(i, carry):
        consume(i)
        return carry

    lax.fori_loop(turns - 2, turns, last, 0)

    landed = hacc[: rows * STEPS, :] + hacc[rows * STEPS :, :]
    landed = jnp.concatenate([landed[r * STEPS : (r + 1) * STEPS, :] for r in range(rows)], axis=1)
    first = four_terms(acc[...] - dot(stack_hi_lo(landed), mp2[...], NT))
    mine = dot(stack_hi_lo(first), slot_own.astype(BF16))
    fst[me] = mine[:STEPS] + mine[STEPS:]
    for j in range(1, rows):
        fst_copy(me, j - 1, lax.rem(me + j, rows)).start()

    for j in range(1, zn):
        zb = lax.rem(z + j, zn)
        elem_copy(zb * 2 + c, 0, partner).wait_recv()
        elem_copy(zb * 2 + c, zb, partner).start()
    for j in range(zn):
        elem_copy(lax.rem(z + j, zn) * 2 + (1 - c), 0, partner).wait_recv()

    w = elem[...].reshape(total, total)
    self_row = jnp.sum(jnp.where(iota((total, total), 0) == iota((total, total), 1), w, 0.0), axis=0, keepdims=True)
    w_hi, w_lo = hi_lo(jnp.transpose(w))
    wc[:, :total] = w_hi
    wc[:, total:] = w_lo

    full = (8, total)
    is_arrest = iota(full, 1) % elems < arrests
    arrest_gain = jnp.where(is_arrest, jnp.broadcast_to(all_par[1:2, :], full), 0.0)
    core_gain = jnp.where(is_arrest, 0.0, jnp.broadcast_to(all_par[2:3, :], full))
    elem_self = jnp.broadcast_to(self_row, full)
    volts0 = jnp.broadcast_to(all_par[3:4, :], full)
    flux0 = jnp.broadcast_to(all_par[4:5, :], full)
    put = jnp.where(jnp.logical_and(at_slot, owner_of == me), 1.0, 0.0).astype(BF16)
    here = dot(jnp.ones((8, total), BF16), put, NT)[0:1]

    for j in range(1, subs):
        sub_copy(j).wait_send()
    for k in range(CHUNKS):
        @pl.when(z + 1 < zn)
        def _():
            line_copy(k, me, 0, partner).wait_send()

        @pl.when(z > 0)
        def _():
            line_copy(k, me, 1, partner).wait_send()

        line_copy(k, me, 2, partner).wait_send()

    def drain(i, carry):
        zb, zt, valid, onward = turn(i)
        b = zb * 2 + c

        @pl.when(valid)
        def _():
            for kind in range(CHUNKS):
                @pl.when(onward)
                def _():
                    line_copy(kind, b, 0, partner).wait_send()

                line_copy(kind, b, 2, partner).wait_send()

        return carry

    lax.fori_loop(0, turns, drain, 0)
    for j in range(1, rows):
        par_copy(me, j - 1, partner).wait_send()
    for at in range(2 * zn - 1):
        rec_copy(me, at, partner).wait_send()
        elem_copy(me, at, partner).wait_send()

    for j in range(1, rows):
        fst_copy(lax.rem(me + j, rows), j - 1, partner).wait_recv()
    fall[...] = jnp.concatenate(
        [sum(fst[h * group + i] for i in range(group)) for h in range(halves)], axis=1
    )

    def advance(t, carry):
        voltage, flux_now = carry
        first_now = jnp.broadcast_to(fall[pl.ds(t, 1), :], full)
        iterate = voltage
        for newton_pass in range(NEWTON):
            linked = flux_now + half_step * (iterate + voltage)
            ratio = iterate * (1.0 / knee_volts)
            rr = ratio * ratio
            ll = linked * linked
            current = arrest_gain * (iterate * (1.0 + rr)) + core_gain * (linked * (1.0 + cubic_term * ll))
            slope = arrest_gain * (1.0 + 3.0 * rr) + core_gain * (half_step + (half_step * 3.0 * cubic_term) * ll)
            recip = 1.0 / (1.0 + elem_self * slope)
            got = dot(stack_hi_lo(current), wc[...])
            coupled = got[:8, :total] + got[8:, :total] + got[:8, total:]
            iterate = iterate - (iterate - first_now + coupled) * recip
        vo[pl.ds(t, 1), :] = iterate[0:1]
        cu[pl.ds(t, 1), :] = current[0:1]
        return iterate, flux_now + half_step * (iterate + voltage)

    lax.fori_loop(0, STEPS, advance, (volts0, flux0), unroll=4)

    reach = four_terms(dot(stack_hi_lo(cu[...]), x2[...], NT))
    placed = dot(stack_hi_lo(vo[...]), put, NT)
    stacked = jnp.where(here > 0.5, placed[:STEPS] + placed[STEPS:], first - reach)
    out[:STEPS, :] = stacked
    summed = jnp.sum(stacked, axis=0, keepdims=True)
    last_flux = flux[...] + half_step * (prev[...] + 2.0 * summed - stacked[STEPS - 1 : STEPS])
    out[STEPS:, :] = jnp.broadcast_to(last_flux, (8, ports))
    for j in range(1, rows):
        fst_copy(me, j - 1, partner).wait_send()


def give(both, volts, last_flux):
    volts[0] = both[:STEPS, :]
    last_flux[...] = both[STEPS : STEPS + 1, :]


def on_device(subs, rows, *args):
    inverse, sources = args[0], args[1]
    ports = inverse.shape[1]
    order = inverse.shape[2]
    slice_len = sources.shape[2]
    arrests, cores = args[10].shape[1], args[11].shape[1]
    elems = arrests + cores
    total = rows * elems
    zn = rows // 2
    tag_rows = -(-2 * (subs - 1) // 8) * 8
    vmem = pl.BlockSpec(memory_space=pltpu.VMEM)
    hbm = pl.BlockSpec(memory_space=pl.ANY)
    dma = pltpu.SemaphoreType.DMA
    small = args[2:]
    both = pl.pallas_call(
        functools.partial(kernel, subs, rows, ports, slice_len, arrests, cores, len(small)),
        out_shape=jax.ShapeDtypeStruct((STEPS + 8, ports), F32),
        in_specs=[hbm] * len(args),
        out_specs=vmem,
        scratch_shapes=[pltpu.VMEM(a.shape, a.dtype) for a in small]
        + [
            pltpu.VMEM((ports, order), F32),
            pltpu.VMEM((2 * ports, order), BF16),
            pltpu.VMEM((ports, rows * ports), F32),
            pltpu.VMEM((2 * ports, rows * ports), BF16),
            pltpu.VMEM((CHUNKS, rows, STEPS, slice_len // CHUNKS), F32),
            pltpu.VMEM((subs - 1, STEPS + 8, LANES), F32),
            pltpu.VMEM((rows, (subs - 1) * STEPS + tag_rows, LANES), F32),
            pltpu.VMEM((rows, elems, total), F32),
            pltpu.VMEM((rows, 8, LANES), F32),
            pltpu.VMEM((rows, STEPS, LANES), F32),
            pltpu.VMEM((STEPS + 8, LANES), F32),
            pltpu.VMEM((2 * ports, total), BF16),
            pltpu.VMEM((total, 2 * total), BF16),
            pltpu.VMEM((STEPS, total), F32),
            pltpu.VMEM((STEPS, total), F32),
            pltpu.VMEM((STEPS, total), F32),
            pltpu.VMEM((2 * STEPS, 2 * ports), F32),
            pltpu.VMEM((2 * STEPS * rows, ports), F32),
            dma((len(small),)),
            dma((rows,)),
            dma((rows,)),
            dma((CHUNKS,)),
            dma((CHUNKS, rows, 3)),
            dma((CHUNKS, rows)),
            dma((subs - 1,)),
            dma((subs - 1,)),
            dma((2 * zn - 1,)),
            dma((rows,)),
            dma((rows - 1,)),
            dma((rows,)),
            dma((2 * zn - 1,)),
            dma((rows,)),
            dma((rows - 1,)),
            dma((rows,)),
        ],
        compiler_params=pltpu.CompilerParams(collective_id=0, has_side_effects=True),
        name="window",
    )(*args)
    return pl.pallas_call(
        give,
        out_shape=(
            jax.ShapeDtypeStruct((1, STEPS, ports), F32),
            jax.ShapeDtypeStruct((1, ports), F32),
        ),
        in_specs=[vmem],
        out_specs=(vmem, vmem),
        name="give",
    )(both)


def solution(mesh):
    subs, rows = mesh.shape["sub"], mesh.shape["row"]
    in_specs = (
        P("sub", "row", None),
        P("sub", None, "row"),
        P("sub", None, "row"),
    ) + (P("sub", "row"),) * 9
    out_specs = (P("sub", None, "row"), P("sub", "row"))
    return jax.shard_map(
        functools.partial(on_device, subs, rows),
        mesh=mesh, in_specs=in_specs, out_specs=out_specs, check_vma=False,
    )
```
